32 devices in a mesh: comp: 8 (over z, y), harm: 4 (over x, core).
Axes of the slice: x: 2, y: 2, z: 4, core: 2. Of those that a mesh axis runs over, the one named last changes fastest.
Arguments:
- load: float32 [128, 32768], P('harm', 'comp'), may hold values from -6 to 6
- stiff_blocks: bfloat16 [256, 8, 128, 128], P('comp'), as said below
- mass_blocks: bfloat16 [256, 8, 128, 128], P('comp'), as said below
- block_cols: int32 [256, 8], P('comp'), may hold values from -8 to 263, as said below
- contact_rows: int32 [8, 256], P('comp'), may hold values from 0 to 4095, as said below
- partner_slot: int32 [8, 256], P('comp'), may hold values from 0 to 255, each once within a row
- contact_count: int32 [8], P('comp'), may hold values from 32 to 256, as said below
- normal_load: float32 [8, 256], P('comp'), may hold values from 0.3 to 3
- contact_stiffness: float32 [8, 256], P('comp'), may hold values from 0.3 to 3
- frequency: float32 [1], replicated, may hold values from 0.2 to 1
Outputs:
- displacement: float32 [128, 32768], P('harm', 'comp')
- residual: float32 [128, 32768], P('harm', 'comp')
The draws below stay inside these ranges and needn't reach their ends.
Inputs may be any that keep to these rules, and one draw needn't show every extreme that they name: `block_cols`: entry 0 of block row r is r; its other 7 entries are distinct, differ from r by 1 to 8, and include r - 8 and r + 8; columns outside 0 .. 255 refer to zero parts of the field. `contact_rows`: the 256 entries of one group are distinct. Slots 0 .. contact_count[d]-1 of group d are live; the others carry no force. `stiff_blocks`: slot 0 of every block row is the block on the diagonal. `mass_blocks`: slot 0 of every block row is the block on the diagonal.
All inputs are finite; a program needn't handle non-finite values.
Results may differ from the reference program's by a relative error of at most 0.015.
The reference program's roundings to bfloat16 on the way (of `rounded`) count: a program that leaves them out, or rounds other values in their place, can miss the bound.
Values may be sent and summed in bfloat16 or wider, within the bound.
A program may use at most 64 MiB of HBM per device.

```python
import math
import jax
import jax.numpy as jnp
from jax import lax

H = 128
TIME_POINTS = 1024
BLK = 128
SLOTS = 8
BAND = 8
ITERS = 3
CMAX = 256
GROUPS = 8
NB = 256
DOF_DEV = 4096
NDOF = 32768


def block_draw(key, lowest, highest, spread):
    key_one, key_two = jax.random.split(key)
    values = jnp.clip(jax.random.normal(key_one, (NB, SLOTS, BLK, BLK), jnp.float32), -6.0, 6.0)
    values = values * (spread / math.sqrt(SLOTS * BLK))
    diagonal = jax.random.uniform(key_two, (NB, BLK), jnp.float32, lowest, highest)
    values = values.at[:, 0].add(diagonal[:, :, None] * jnp.eye(BLK, dtype=jnp.float32)[None, :, :])
    return values.astype(jnp.bfloat16)


def draw_stiff_blocks(key, part):
    return block_draw(jax.random.fold_in(key, 11), 3.0, 5.0, 1.0)


def draw_mass_blocks(key, part):
    return block_draw(jax.random.fold_in(key, 23), 0.5, 1.0, 0.25)


def draw_block_cols(key, part):
    row_ids = jnp.arange(NB, dtype=jnp.int32)
    offset_pool = jnp.concatenate([jnp.arange(1 - BAND, 0, dtype=jnp.int32), jnp.arange(1, BAND, dtype=jnp.int32)])

    def one_row(row_key):
        pick_key, order_key = jax.random.split(row_key)
        picked = jax.random.permutation(pick_key, offset_pool)[:SLOTS - 3]
        others = jnp.concatenate([jnp.array([-BAND, BAND], jnp.int32), picked])
        return jnp.concatenate([jnp.zeros((1,), jnp.int32), jax.random.permutation(order_key, others)])
    offsets = jax.vmap(one_row)(jax.random.split(jax.random.fold_in(key, 31), NB))
    return row_ids[:, None] + offsets


def draw_contact_rows(key, part):
    key_one, key_two = jax.random.split(jax.random.fold_in(key, 41))
    inner_rows = jnp.arange(1, DOF_DEV - 1, dtype=jnp.int32)

    def one_device(device_key):
        pick_key, order_key, drawn_key = jax.random.split(device_key, 3)
        drawn_rows = jax.random.permutation(drawn_key, jnp.arange(DOF_DEV, dtype=jnp.int32))[:CMAX]
        chosen = jax.random.permutation(pick_key, inner_rows)[:CMAX - 2]
        with_ends = jnp.concatenate([jnp.array([0, DOF_DEV - 1], jnp.int32), chosen])
        return (drawn_rows, jax.random.permutation(order_key, with_ends))
    drawn_rows, ended = jax.vmap(one_device)(jax.random.split(key_one, GROUPS))
    marked = jax.random.randint(key_two, (), 0, GROUPS)
    return jnp.where((jnp.arange(GROUPS, dtype=jnp.int32) == marked)[:, None], ended, drawn_rows)


def draw_contact_count(key, part):
    key_one, key_two, key_three, key_four = jax.random.split(jax.random.fold_in(key, 53), 4)
    counts = jax.random.randint(key_one, (GROUPS,), CMAX // 8, CMAX // 2 + 1)
    heavy = jax.random.randint(key_two, (GROUPS,), 0, 8) == 0
    counts = jnp.where(heavy, CMAX, counts)
    busiest = jax.random.randint(key_three, (), 0, GROUPS)
    lightest = (busiest + 1 + jax.random.randint(key_four, (), 0, GROUPS - 1)) % GROUPS
    counts = counts.at[busiest].set(CMAX).at[lightest].set(CMAX // 8)
    return counts.astype(jnp.int32)


def block_levels(key, dims, pieces, low, largest):
    loudness, own = 1.0, jax.random.fold_in(key, 6)
    for axis_at, parts in pieces:
        draws = jnp.exp(jax.random.uniform(jax.random.fold_in(own, axis_at), (parts,), jnp.float32, low / len(pieces), largest / len(pieces)))
        loudness = loudness * jnp.repeat(draws, dims[axis_at] // parts).reshape([-1 if axis == axis_at else 1 for axis in range(len(dims))])
    return loudness


def centred(key, extent, width, most, cuts=(), held_as=jnp.bfloat16):
    entries = width * jax.random.normal(key, extent, jnp.float32)
    if cuts:
        entries = entries * block_levels(key, extent, cuts, -0.22, 0.18)
    return jnp.clip(entries, -most, most).astype(held_as)


def setup_inputs(seed: int = 0) -> dict:
    splits = jax.random.split(jax.random.key(seed), 11)
    load = centred(splits[0], (H, NDOF), 1.0, 6.0, ((0, 4), (1, 8)), jnp.float32)
    stiff_blocks = draw_stiff_blocks(jax.random.fold_in(splits[10], 71), 0)
    mass_blocks = draw_mass_blocks(jax.random.fold_in(splits[10], 71), 0)
    block_cols = draw_block_cols(jax.random.fold_in(splits[10], 71), 0)
    contact_rows = draw_contact_rows(jax.random.fold_in(splits[10], 71), 0)
    partner_slot = jax.vmap(lambda own: jax.random.permutation(own, CMAX))(jax.random.split(splits[5], GROUPS)).reshape((GROUPS, CMAX)).astype(jnp.int32)
    contact_count = draw_contact_count(jax.random.fold_in(splits[10], 71), 0)
    normal_load = jnp.clip(jnp.exp(math.log(3.0) - 2.3025851 * jax.random.uniform(splits[7], (GROUPS, CMAX), jnp.float32) ** block_levels(splits[7], (GROUPS, CMAX), ((0, 8),), -0.2, 0.2)), 0.3, 3.0)
    contact_stiffness = jnp.clip(jnp.exp(math.log(3.0) - 2.3025851 * jax.random.uniform(splits[8], (GROUPS, CMAX), jnp.float32) ** block_levels(splits[8], (GROUPS, CMAX), ((0, 8),), -0.2, 0.2)), 0.3, 3.0)
    frequency = jnp.clip(jax.random.uniform(splits[9], (1,), jnp.float32, 0.2, 1.0), 0.2, 1.0)
    return dict(load=load, stiff_blocks=stiff_blocks, mass_blocks=mass_blocks, block_cols=block_cols, contact_rows=contact_rows, partner_slot=partner_slot, contact_count=contact_count, normal_load=normal_load, contact_stiffness=contact_stiffness, frequency=frequency)


def harmonic_tables():
    column_list = jnp.arange(H, dtype=jnp.int32)
    harmonic_orders = jnp.where(column_list <= H // 2, column_list, column_list - H // 2).astype(jnp.int32)
    time_points = jnp.arange(TIME_POINTS, dtype=jnp.int32)
    phase_values = (time_points[:, None] * harmonic_orders[None, :]) % TIME_POINTS
    phase_angles = phase_values.astype(jnp.float32) * jnp.float32(2.0 * math.pi / TIME_POINTS)
    instant_table = jnp.where(column_list[None, :] <= H // 2, jnp.cos(phase_angles), jnp.sin(phase_angles))
    weight_factors = jnp.where(column_list == 0, jnp.float32(1.0), jnp.float32(2.0)).astype(jnp.float32) / jnp.float32(TIME_POINTS)
    return instant_table, weight_factors, harmonic_orders


def block_products(stiff_blocks, mass_blocks, block_cols, rounded):
    padded = jnp.pad(rounded.reshape(H, NB, BLK), ((0, 0), (BAND, BAND), (0, 0))).astype(jnp.float32)

    def one_row(row_index):
        stiff_row = stiff_blocks[row_index].astype(jnp.float32)
        mass_row = mass_blocks[row_index].astype(jnp.float32)
        column_row = (block_cols[row_index] + BAND).astype(jnp.int32)
        picked = jnp.take(padded, column_row, axis=1)
        stiff_out = jnp.einsum("sij,hsj->hi", stiff_row, picked, precision=lax.Precision.HIGHEST)
        mass_out = jnp.einsum("sij,hsj->hi", mass_row, picked, precision=lax.Precision.HIGHEST)
        return stiff_out, mass_out

    stiff_all, mass_all = lax.map(one_row, jnp.arange(NB, dtype=jnp.int32))
    stiff_part = jnp.transpose(stiff_all, (1, 0, 2)).reshape(H, NB * BLK)
    mass_part = jnp.transpose(mass_all, (1, 0, 2)).reshape(H, NB * BLK)
    return stiff_part, mass_part


def contact_force(displacement, contact_rows, partner_slot, contact_count, normal_load, contact_stiffness, instant_table, weight_factors):
    shaped = displacement.reshape(H, GROUPS, DOF_DEV)
    listed = jnp.take_along_axis(shaped, contact_rows[None, :, :].astype(jnp.int32), axis=2)
    partner_ids = jnp.bitwise_xor(jnp.arange(GROUPS, dtype=jnp.int32), jnp.int32(GROUPS // 2))
    facing = jnp.take_along_axis(jnp.take(listed, partner_ids, axis=1), partner_slot[None, :, :].astype(jnp.int32), axis=2)
    relative = (listed - facing).reshape(H, GROUPS * CMAX)
    time_values = jnp.dot(instant_table, relative, precision=lax.Precision.HIGHEST)
    load_part = normal_load.reshape(1, GROUPS * CMAX)
    stiff_part = contact_stiffness.reshape(1, GROUPS * CMAX)
    live_mask = (jnp.arange(CMAX, dtype=jnp.int32)[None, :] < contact_count[:, None]).reshape(1, GROUPS * CMAX)
    forces = jnp.where(live_mask, load_part * jnp.tanh(stiff_part * time_values / load_part), jnp.zeros_like(time_values))
    projected = lax.dot_general(instant_table, forces, (((0,), (0,)), ((), ())), precision=lax.Precision.HIGHEST) * weight_factors[:, None]
    targets = (jnp.arange(GROUPS, dtype=jnp.int32)[:, None] * DOF_DEV + contact_rows.astype(jnp.int32)).reshape(GROUPS * CMAX)
    return jnp.zeros((H, NDOF), projected.dtype).at[:, targets].add(projected)


def reference(load, stiff_blocks, mass_blocks, block_cols, contact_rows, partner_slot, contact_count, normal_load, contact_stiffness, frequency):
    instant_table, weight_factors, harmonic_orders = harmonic_tables()
    factor = frequency[0] * harmonic_orders.astype(jnp.float32) * jnp.float32(2.0 / H)
    factor = factor * factor
    stiff_diag = jnp.diagonal(stiff_blocks[:, 0], axis1=1, axis2=2).astype(jnp.float32).reshape(NDOF)
    mass_diag = jnp.diagonal(mass_blocks[:, 0], axis1=1, axis2=2).astype(jnp.float32).reshape(NDOF)
    dynamic = stiff_diag[None, :] - factor[:, None] * mass_diag[None, :]
    displacement = load / dynamic
    residual = jnp.zeros_like(displacement)
    for sweep_index in range(ITERS):
        rounded = displacement.astype(jnp.bfloat16)
        gap = displacement - lax.optimization_barrier(rounded).astype(jnp.float32)
        stiff_part, mass_part = block_products(stiff_blocks, mass_blocks, block_cols, rounded)
        stiff_part = stiff_part + stiff_diag[None, :] * gap
        mass_part = mass_part + mass_diag[None, :] * gap
        applied = stiff_part - factor[:, None] * mass_part
        nonlinear = contact_force(displacement, contact_rows, partner_slot, contact_count, normal_load, contact_stiffness, instant_table, weight_factors)
        residual = load - applied - nonlinear
        displacement = displacement + residual / dynamic
    return displacement, residual
```

```python
import functools
import math

import jax
import jax.numpy as jnp
import numpy as np
from jax import lax
from jax.experimental import pallas as pl
from jax.experimental.pallas import tpu as pltpu
from jax.sharding import PartitionSpec as P

H = 128
TIME_POINTS = 1024
BAND = 8
ITERS = 3
MESH = pl.DeviceIdType.MESH
F32 = jnp.float32
BF16 = jnp.bfloat16
NN = (((1,), (0,)), ((), ()))
NT = (((1,), (1,)), ((), ()))


def host_tables(harm_parts):
    column = np.arange(H)
    orders = np.where(column <= H // 2, column, column - H // 2)
    phase = np.arange(TIME_POINTS)[:, None] * orders[None, :] % TIME_POINTS
    angle = phase * (2.0 * math.pi / TIME_POINTS)
    table = np.where(column[None, :] <= H // 2, np.cos(angle), np.sin(angle))
    table = table.astype(np.float32)
    high = table.astype(BF16)
    low = (table - high.astype(np.float32)).astype(BF16)
    to_time = np.concatenate([high, low], axis=1)
    back = np.stack(
        [high.T.reshape(harm_parts, -1, TIME_POINTS), low.T.reshape(harm_parts, -1, TIME_POINTS)], axis=1
    )
    return to_time, back.reshape(harm_parts, -1, TIME_POINTS)


def halves(value):
    high = value.astype(BF16)
    low = (value - high.astype(F32)).astype(BF16)
    return high, low


def stacked(value):
    return jnp.concatenate(halves(value), axis=0)


def folded(value):
    half = value.shape[0] // 2
    return value[:half] + value[half:]


def product(left, right, dims):
    return lax.dot_general(left, right, dims, preferred_element_type=F32)


def kernel(
    comp_size,
    harm_size,
    load_ref,
    stiff_hbm,
    mass_hbm,
    cols_ref,
    rows_ref,
    partner_ref,
    count_ref,
    normal_ref,
    spring_ref,
    freq_ref,
    time_ref,
    back_ref,
    disp_out,
    res_out,
    stiff_ref,
    mass_ref,
    field,
    shift,
    dyn_ref,
    hot,
    perm,
    ext,
    halo,
    swap_out,
    swap_in,
    shared,
    rel_high,
    rel_low,
    diag_sem,
    block_sem,
    halo_send,
    halo_recv,
    swap_send,
    swap_recv,
    share_send,
    share_recv,
):
    comp = lax.axis_index("comp")
    harm = lax.axis_index("harm")
    block_rows = stiff_ref.shape[0]
    slots = stiff_ref.shape[1]
    blk = stiff_ref.shape[2]
    nh = load_ref.shape[0]
    wide = 2 * blk
    pairs = block_rows // 2
    chunks = block_rows // BAND
    cmax = rows_ref.shape[1]
    first_row = comp * block_rows
    has_prev = comp > 0
    has_next = comp < comp_size - 1
    after = lax.rem(comp + 1, comp_size)
    before = lax.rem(comp + comp_size - 1, comp_size)
    facing = lax.rem(comp + comp_size // 2, comp_size)
    order = list(range(1, chunks - 1)) + [0, chunks - 1]

    diag_copies = [
        pltpu.make_async_copy(source.at[:, pl.ds(0, 1)], held.at[:, pl.ds(0, 1)], diag_sem.at[i])
        for i, (source, held) in enumerate(((stiff_hbm, stiff_ref), (mass_hbm, mass_ref)))
    ]
    for copy in diag_copies:
        copy.start()
    block_copies = {}
    for c in order:
        span = (pl.ds(c * BAND, BAND), pl.ds(1, slots - 1))
        block_copies[c] = [
            pltpu.make_async_copy(source.at[span], held.at[span], block_sem.at[c, i])
            for i, (source, held) in enumerate(((stiff_hbm, stiff_ref), (mass_hbm, mass_ref)))
        ]
        for copy in block_copies[c]:
            copy.start()

    barrier = pltpu.get_barrier_semaphore()
    pl.semaphore_signal(barrier, inc=1, device_id=(facing, harm), device_id_type=MESH)
    for step in range(1, harm_size):
        peer = lax.rem(harm + step, harm_size)
        pl.semaphore_signal(barrier, inc=1, device_id=(comp, peer), device_id_type=MESH)

    @pl.when(has_prev)
    def _():
        pl.semaphore_signal(barrier, inc=1, device_id=(before, harm), device_id_type=MESH)

    @pl.when(has_next)
    def _():
        pl.semaphore_signal(barrier, inc=1, device_id=(after, harm), device_id_type=MESH)

    row_list = rows_ref[...]
    sub = lax.broadcasted_iota(jnp.int32, (wide, cmax), 0)

    def mark(p, carry):
        base = pl.multiple_of(p * wide, wide)
        hot[pl.ds(base, wide), :] = jnp.where(sub == row_list - base, 1.0, 0.0).astype(BF16)
        return carry

    lax.fori_loop(0, pairs, mark, 0)
    slot_axis = lax.broadcasted_iota(jnp.int32, (cmax, cmax), 0)
    perm[...] = jnp.where(slot_axis == partner_ref[...], 1.0, 0.0).astype(BF16)
    ext[pl.ds(0, BAND)] = jnp.zeros((BAND, nh, blk), BF16)
    ext[pl.ds(BAND + block_rows, BAND)] = jnp.zeros((BAND, nh, blk), BF16)

    def factor_of(width):
        index = harm * nh + lax.broadcasted_iota(jnp.int32, (nh, width), 0)
        wave = jnp.where(index <= H // 2, index, index - H // 2).astype(F32)
        value = freq_ref[0] * wave * (2.0 / H)
        return value * value

    slot_index = lax.broadcasted_iota(jnp.int32, (1, cmax), 1)
    slot_scale = jnp.where(slot_index < count_ref[0], normal_ref[...], 0.0)
    own_index = harm * nh + lax.broadcasted_iota(jnp.int32, (nh, cmax), 0)
    own_weight = jnp.where(own_index == 0, 1.0 / TIME_POINTS, 2.0 / TIME_POINTS)
    spring_ratio = spring_ref[...] / normal_ref[...]

    for copy in diag_copies:
        copy.wait()
    eye = lax.broadcasted_iota(jnp.int32, (blk, blk), 0) == lax.broadcasted_iota(
        jnp.int32, (blk, blk), 1
    )

    def diagonal(ref, p):
        parts = [
            jnp.sum(jnp.where(eye, ref[2 * p + q, 0].astype(F32), 0.0), axis=0, keepdims=True)
            for q in range(2)
        ]
        return jnp.concatenate(parts, axis=1)

    def put_rounded(p, value):
        rounded = value.astype(BF16)
        for q in range(2):
            ext[BAND + 2 * p + q] = rounded[:, q * blk : (q + 1) * blk]

    def lanes(p):
        return pl.ds(pl.multiple_of(p * wide, wide), wide)

    def start_field(p, listed):
        dynamic = diagonal(stiff_ref, p) - factor_of(wide) * diagonal(mass_ref, p)
        value = load_ref[:, lanes(p)] / dynamic
        dyn_ref[p] = dynamic
        field[p] = value
        put_rounded(p, value)
        return listed + product(stacked(value), hot[lanes(p), :], NN)

    listed = lax.fori_loop(0, pairs, start_field, jnp.zeros((2 * nh, cmax), F32))

    neighbours = jnp.minimum(comp, 1) + jnp.minimum(comp_size - 1 - comp, 1)
    pl.semaphore_wait(barrier, harm_size + neighbours)

    def apply_rows(chunk):
        def body(p, carry):
            applied = []
            for q in range(2):
                r = 2 * p + q
                picked = jnp.concatenate(
                    [
                        ext[jnp.clip(cols_ref[r, s] - first_row + BAND, 0, ext.shape[0] - 1)]
                        for s in range(slots)
                    ],
                    axis=1,
                )
                blocks = jnp.concatenate(
                    [
                        jnp.concatenate([ref[r, s] for s in range(slots)], axis=1)
                        for ref in (stiff_ref, mass_ref)
                    ],
                    axis=0,
                )
                both = product(picked, blocks, NT)
                applied.append(both[:, :blk] - factor_of(blk) * both[:, blk:])
            rounded = jnp.concatenate([ext[BAND + 2 * p + q] for q in range(2)], axis=1)
            gap = field[p] - rounded.astype(F32)
            shift[p] = (
                load_ref[:, lanes(p)] - jnp.concatenate(applied, axis=1) - dyn_ref[p] * gap
            )
            return carry

        lax.fori_loop(chunk * BAND // 2, (chunk + 1) * BAND // 2, body, 0)

    for k in range(ITERS):
        up = pltpu.make_async_remote_copy(
            src_ref=ext.at[pl.ds(block_rows, BAND)],
            dst_ref=halo.at[k, 0],
            send_sem=halo_send.at[k, 0],
            recv_sem=halo_recv.at[k, 0],
            device_id=(after, harm),
            device_id_type=MESH,
        )
        down = pltpu.make_async_remote_copy(
            src_ref=ext.at[pl.ds(BAND, BAND)],
            dst_ref=halo.at[k, 1],
            send_sem=halo_send.at[k, 1],
            recv_sem=halo_recv.at[k, 1],
            device_id=(before, harm),
            device_id_type=MESH,
        )
        own = folded(listed)
        swap_out[k] = own
        swap = pltpu.make_async_remote_copy(
            src_ref=swap_out.at[k],
            dst_ref=swap_in.at[k],
            send_sem=swap_send.at[k],
            recv_sem=swap_recv.at[k],
            device_id=(facing, harm),
            device_id_type=MESH,
        )
        swap.start()

        @pl.when(has_next)
        def _():
            up.start()

        @pl.when(has_prev)
        def _():
            down.start()

        def ready(chunk):
            if k == 0:
                for copy in block_copies[chunk]:
                    copy.wait()

        ready(order[0])
        apply_rows(order[0])

        swap.wait()
        mirrored = folded(product(stacked(swap_in[k]), perm[...], NN))
        shared[k, harm] = (swap_out[k] - mirrored) * spring_ratio
        sends = []
        for step in range(1, harm_size):
            sends.append(
                pltpu.make_async_remote_copy(
                    src_ref=shared.at[k, harm],
                    dst_ref=shared.at[k, harm],
                    send_sem=share_send.at[k, step - 1],
                    recv_sem=share_recv.at[k, step - 1],
                    device_id=(comp, lax.rem(harm + step, harm_size)),
                    device_id_type=MESH,
                )
            )
            sends[-1].start()

        for chunk in order[1:-2]:
            ready(chunk)
            apply_rows(chunk)

        @pl.when(has_next)
        def _():
            up.wait_send()
            down.wait_recv()
            ext[pl.ds(BAND + block_rows, BAND)] = halo[k, 1]

        @pl.when(has_prev)
        def _():
            down.wait_send()
            up.wait_recv()
            ext[pl.ds(0, BAND)] = halo[k, 0]

        for chunk in order[-2:]:
            ready(chunk)
            apply_rows(chunk)

        for send in sends:
            send.wait()
        for part in range(harm_size):
            high, low = halves(shared[k, part])
            for copy in range(2):
                rel_high[pl.ds(copy * H + part * nh, nh), :] = high
                rel_low[pl.ds(copy * H + part * nh, nh), :] = low
        total = jnp.zeros((2 * nh, cmax), F32)
        extra = jnp.zeros((nh, cmax), F32)
        step_points = 2 * H
        for t in range(0, TIME_POINTS, step_points):
            rows_now = time_ref[pl.ds(t, step_points), :]
            values = product(rows_now, rel_high[...], NN) + product(rows_now, rel_low[...], NN)
            high, low = halves(jnp.tanh(values))
            back = back_ref[harm, :, pl.ds(t, step_points)]
            total = total + product(back, high, NN)
            extra = extra + product(back[:nh], low, NN)
        projected = stacked((folded(total) + extra) * own_weight * slot_scale)

        last = k == ITERS - 1

        def finish(p, carry):
            nonlinear = folded(product(projected, hot[lanes(p), :], NT))
            residual = shift[p] - nonlinear
            value = field[p] + residual / dyn_ref[p]
            if last:
                disp_out[:, lanes(p)] = value
                res_out[:, lanes(p)] = residual
                return carry
            field[p] = value
            put_rounded(p, value)
            return carry + product(stacked(value), hot[lanes(p), :], NN)

        listed = lax.fori_loop(
            0, pairs, finish, jnp.zeros((8, 128) if last else (2 * nh, cmax), F32)
        )


def local(comp_size, harm_size, *arrays):
    load, stiff_blocks, mass_blocks = arrays[:3]
    nh, dofs = load.shape
    block_rows, slots, blk, _ = stiff_blocks.shape
    cmax = arrays[4].shape[1]
    to_time, back = host_tables(harm_size)
    vmem = pl.BlockSpec(memory_space=pltpu.VMEM)
    smem = pl.BlockSpec(memory_space=pltpu.SMEM)
    hbm = pl.BlockSpec(memory_space=pl.ANY)
    wide = (block_rows // 2, nh, 2 * blk)
    dma = pltpu.SemaphoreType.DMA
    return pl.pallas_call(
        functools.partial(kernel, comp_size, harm_size),
        out_shape=(jax.ShapeDtypeStruct((nh, dofs), F32),) * 2,
        in_specs=[vmem, hbm, hbm, smem, vmem, vmem, smem, vmem, vmem, smem, vmem, vmem],
        out_specs=(vmem, vmem),
        scratch_shapes=[
            pltpu.VMEM(stiff_blocks.shape, BF16),
            pltpu.VMEM(mass_blocks.shape, BF16),
            pltpu.VMEM(wide, F32),
            pltpu.VMEM(wide, F32),
            pltpu.VMEM(wide, F32),
            pltpu.VMEM((dofs, cmax), BF16),
            pltpu.VMEM((cmax, cmax), BF16),
            pltpu.VMEM((block_rows + 2 * BAND, nh, blk), BF16),
            pltpu.VMEM((ITERS, 2, BAND, nh, blk), BF16),
            pltpu.VMEM((ITERS, nh, cmax), F32),
            pltpu.VMEM((ITERS, nh, cmax), F32),
            pltpu.VMEM((ITERS, harm_size, nh, cmax), F32),
            pltpu.VMEM((2 * H, cmax), BF16),
            pltpu.VMEM((2 * H, cmax), BF16),
            dma((2,)),
            dma((block_rows // BAND, 2)),
            dma((ITERS, 2)),
            dma((ITERS, 2)),
            dma((ITERS,)),
            dma((ITERS,)),
            dma((ITERS, harm_size - 1)),
            dma((ITERS, harm_size - 1)),
        ],
        compiler_params=pltpu.CompilerParams(
            collective_id=0, has_side_effects=True, vmem_limit_bytes=56 * 1024 * 1024
        ),
    )(*arrays, jnp.asarray(to_time), jnp.asarray(back))


def solution(mesh):
    placed = (
        P("harm", "comp"),
        P("comp", None, None, None),
        P("comp", None, None, None),
        P("comp", None),
        P("comp", None),
        P("comp", None),
        P("comp"),
        P("comp", None),
        P("comp", None),
        P(),
    )
    return jax.shard_map(
        functools.partial(local, mesh.shape["comp"], mesh.shape["harm"]),
        mesh=mesh,
        in_specs=placed,
        out_specs=(P("harm", "comp"), P("harm", "comp")),
        check_vma=False,
    )
```

```python
import functools
import math

import jax
import jax.numpy as jnp
import numpy as np
from jax import lax
from jax.experimental import pallas as pl
from jax.experimental.pallas import tpu as pltpu
from jax.sharding import PartitionSpec as P

H = 128
TIME_POINTS = 1024
BAND = 8
ITERS = 3
MESH = pl.DeviceIdType.MESH
F32 = jnp.float32
BF16 = jnp.bfloat16
NN = (((1,), (0,)), ((), ()))
NT = (((1,), (1,)), ((), ()))


def host_tables(harm_parts):
    column = np.arange(H)
    orders = np.where(column <= H // 2, column, column - H // 2)
    phase = np.arange(TIME_POINTS)[:, None] * orders[None, :] % TIME_POINTS
    angle = phase * (2.0 * math.pi / TIME_POINTS)
    table = np.where(column[None, :] <= H // 2, np.cos(angle), np.sin(angle))
    table = table.astype(np.float32)
    high = table.astype(BF16)
    low = (table - high.astype(np.float32)).astype(BF16)
    to_time = np.concatenate([high, low], axis=1)
    back = np.stack(
        [high.T.reshape(harm_parts, -1, TIME_POINTS), low.T.reshape(harm_parts, -1, TIME_POINTS)], axis=1
    )
    return to_time, back.reshape(harm_parts, -1, TIME_POINTS)


def halves(value):
    high = value.astype(BF16)
    low = (value - high.astype(F32)).astype(BF16)
    return high, low


def stacked(value):
    return jnp.concatenate(halves(value), axis=0)


def folded(value):
    half = value.shape[0] // 2
    return value[:half] + value[half:]


def product(left, right, dims):
    return lax.dot_general(left, right, dims, preferred_element_type=F32)


def kernel(
    comp_size,
    harm_size,
    load_hbm,
    stiff_hbm,
    mass_hbm,
    cols_ref,
    rows_ref,
    partner_ref,
    count_ref,
    normal_ref,
    spring_ref,
    freq_ref,
    time_hbm,
    back_hbm,
    disp_out,
    res_out,
    load_ref,
    time_ref,
    back_ref,
    stiff_ref,
    mass_ref,
    field,
    shift,
    dyn_ref,
    inv_ref,
    slot_inverse,
    hot,
    perm,
    ext,
    halo,
    swap_out,
    swap_in,
    shared,
    rel_high,
    rel_low,
    side_sem,
    diag_sem,
    block_sem,
    halo_send,
    halo_recv,
    swap_send,
    swap_recv,
    share_send,
    share_recv,
):
    comp = lax.axis_index("comp")
    harm = lax.axis_index("harm")
    block_rows = stiff_ref.shape[0]
    slots = stiff_ref.shape[1]
    blk = stiff_ref.shape[2]
    nh = load_ref.shape[0]
    wide = 2 * blk
    pairs = block_rows // 2
    chunks = block_rows // BAND
    cmax = rows_ref.shape[1]
    first_row = comp * block_rows
    has_prev = comp > 0
    has_next = comp < comp_size - 1
    after = lax.rem(comp + 1, comp_size)
    before = lax.rem(comp + comp_size - 1, comp_size)
    facing = lax.rem(comp + comp_size // 2, comp_size)
    order = list(range(1, chunks - 1)) + [0, chunks - 1]

    diag_copies = [
        pltpu.make_async_copy(source.at[:, pl.ds(0, 1)], held.at[:, pl.ds(0, 1)], diag_sem.at[i])
        for i, (source, held) in enumerate(((stiff_hbm, stiff_ref), (mass_hbm, mass_ref)))
    ]
    for copy in diag_copies:
        copy.start()
    load_copy, *table_copies = [
        pltpu.make_async_copy(source, held, side_sem.at[i])
        for i, (source, held) in enumerate(
            ((load_hbm, load_ref), (time_hbm, time_ref), (back_hbm, back_ref))
        )
    ]
    load_copy.start()
    block_copies = {}
    for c in order:
        span = (pl.ds(c * BAND, BAND), pl.ds(1, slots - 1))
        block_copies[c] = [
            pltpu.make_async_copy(source.at[span], held.at[span], block_sem.at[c, i])
            for i, (source, held) in enumerate(((stiff_hbm, stiff_ref), (mass_hbm, mass_ref)))
        ]
        for copy in block_copies[c]:
            copy.start()
    for copy in table_copies:
        copy.start()

    barrier = pltpu.get_barrier_semaphore()
    pl.semaphore_signal(barrier, inc=1, device_id=(facing, harm), device_id_type=MESH)
    for step in range(1, harm_size):
        peer = lax.rem(harm + step, harm_size)
        pl.semaphore_signal(barrier, inc=1, device_id=(comp, peer), device_id_type=MESH)

    @pl.when(has_prev)
    def _():
        pl.semaphore_signal(barrier, inc=1, device_id=(before, harm), device_id_type=MESH)

    @pl.when(has_next)
    def _():
        pl.semaphore_signal(barrier, inc=1, device_id=(after, harm), device_id_type=MESH)

    row_list = rows_ref[...]
    sub = lax.broadcasted_iota(jnp.int32, (wide, cmax), 0)

    def mark(p, carry):
        base = pl.multiple_of(p * wide, wide)
        hot[pl.ds(base, wide), :] = jnp.where(sub == row_list - base, 1.0, 0.0).astype(BF16)
        return carry

    lax.fori_loop(0, pairs, mark, 0)
    slot_axis = lax.broadcasted_iota(jnp.int32, (cmax, cmax), 0)
    perm[...] = jnp.where(slot_axis == partner_ref[...], 1.0, 0.0).astype(BF16)
    ext[pl.ds(0, BAND)] = jnp.zeros((BAND, nh, blk), BF16)
    ext[pl.ds(BAND + block_rows, BAND)] = jnp.zeros((BAND, nh, blk), BF16)

    def factor_of(width):
        index = harm * nh + lax.broadcasted_iota(jnp.int32, (nh, width), 0)
        wave = jnp.where(index <= H // 2, index, index - H // 2).astype(F32)
        value = freq_ref[0] * wave * (2.0 / H)
        return value * value

    slot_index = lax.broadcasted_iota(jnp.int32, (1, cmax), 1)
    slot_scale = jnp.where(slot_index < count_ref[0], normal_ref[...], 0.0)
    own_index = harm * nh + lax.broadcasted_iota(jnp.int32, (nh, cmax), 0)
    own_weight = jnp.where(own_index == 0, 1.0 / TIME_POINTS, 2.0 / TIME_POINTS)
    spring_ratio = spring_ref[...] / normal_ref[...]

    for copy in diag_copies:
        copy.wait()
    load_copy.wait()
    eye = lax.broadcasted_iota(jnp.int32, (blk, blk), 0) == lax.broadcasted_iota(
        jnp.int32, (blk, blk), 1
    )

    def diagonal(ref, p):
        parts = [
            jnp.sum(jnp.where(eye, ref[2 * p + q, 0].astype(F32), 0.0), axis=0, keepdims=True)
            for q in range(2)
        ]
        return jnp.concatenate(parts, axis=1)

    def put_rounded(p, value):
        rounded = value.astype(BF16)
        for q in range(2):
            ext[BAND + 2 * p + q] = rounded[:, q * blk : (q + 1) * blk]

    def lanes(p):
        return pl.ds(pl.multiple_of(p * wide, wide), wide)

    def start_field(p, gathered):
        stiff_diag = diagonal(stiff_ref, p)
        mass_diag = diagonal(mass_ref, p)
        dynamic = stiff_diag - factor_of(wide) * mass_diag
        value = load_ref[:, lanes(p)] / dynamic
        dyn_ref[p] = dynamic
        inv_ref[p] = 1.0 / dynamic
        field[p] = value
        put_rounded(p, value)
        high, low = halves(value)
        diagonals = jnp.concatenate(
            [jnp.broadcast_to(part, (8, wide)) for part in (stiff_diag, mass_diag)], axis=0
        )
        left = jnp.concatenate([high, low, diagonals.astype(BF16)], axis=0)
        return gathered + product(left, hot[lanes(p), :], NN)

    gathered = lax.fori_loop(
        0, pairs, start_field, jnp.zeros((2 * nh + 16, cmax), F32), unroll=2
    )
    listed = folded(gathered[: 2 * nh])
    slot_dynamic = gathered[2 * nh : 2 * nh + 1] - factor_of(cmax) * gathered[2 * nh + 8 : 2 * nh + 9]
    slot_inverse[...] = 1.0 / slot_dynamic

    neighbours = jnp.minimum(comp, 1) + jnp.minimum(comp_size - 1 - comp, 1)
    pl.semaphore_wait(barrier, harm_size + neighbours)

    def apply_rows(first, stop, gathered):
        def body(p, carry):
            applied = []
            for q in range(2):
                r = 2 * p + q
                picked = jnp.concatenate(
                    [
                        ext[jnp.clip(cols_ref[s, r] - first_row + BAND, 0, ext.shape[0] - 1)]
                        for s in range(slots)
                    ],
                    axis=1,
                )
                blocks = jnp.concatenate(
                    [
                        jnp.concatenate([ref[r, s] for s in range(slots)], axis=1)
                        for ref in (stiff_ref, mass_ref)
                    ],
                    axis=0,
                )
                both = product(picked, blocks, NT)
                applied.append(both[:, :blk] - factor_of(blk) * both[:, blk:])
            rounded = jnp.concatenate([ext[BAND + 2 * p + q] for q in range(2)], axis=1)
            gap = field[p] - rounded.astype(F32)
            value = load_ref[:, lanes(p)] - jnp.concatenate(applied, axis=1) - dyn_ref[p] * gap
            shift[p] = value
            if carry is None:
                return carry
            return carry + product(stacked(value), hot[lanes(p), :], NN)

        return lax.fori_loop(first * BAND // 2, stop * BAND // 2, body, gathered, unroll=2)

    def swap_copy(k):
        return pltpu.make_async_remote_copy(
            src_ref=swap_out.at[k],
            dst_ref=swap_in.at[k],
            send_sem=swap_send.at[k],
            recv_sem=swap_recv.at[k],
            device_id=(facing, harm),
            device_id_type=MESH,
        )

    swap_out[0] = listed
    swap_copy(0).start()

    for k in range(ITERS):
        up = pltpu.make_async_remote_copy(
            src_ref=ext.at[pl.ds(block_rows, BAND)],
            dst_ref=halo.at[k, 0],
            send_sem=halo_send.at[k, 0],
            recv_sem=halo_recv.at[k, 0],
            device_id=(after, harm),
            device_id_type=MESH,
        )
        down = pltpu.make_async_remote_copy(
            src_ref=ext.at[pl.ds(BAND, BAND)],
            dst_ref=halo.at[k, 1],
            send_sem=halo_send.at[k, 1],
            recv_sem=halo_recv.at[k, 1],
            device_id=(before, harm),
            device_id_type=MESH,
        )
        @pl.when(has_next)
        def _():
            up.start()

        @pl.when(has_prev)
        def _():
            down.start()

        last = k == ITERS - 1

        def span(first, stop, gathered):
            if k > 0:
                return apply_rows(first, stop, gathered)
            for chunk in range(first, stop):
                for copy in block_copies[chunk]:
                    copy.wait()
                gathered = apply_rows(chunk, chunk + 1, gathered)
            return gathered

        gathered = None if last else jnp.zeros((2 * nh, cmax), F32)
        gathered = span(1, chunks - 1, gathered)

        swap_copy(k).wait()
        mirrored = folded(product(stacked(swap_in[k]), perm[...], NN))
        shared[k, harm] = (swap_out[k] - mirrored) * spring_ratio
        sends = []
        for step in range(1, harm_size):
            sends.append(
                pltpu.make_async_remote_copy(
                    src_ref=shared.at[k, harm],
                    dst_ref=shared.at[k, harm],
                    send_sem=share_send.at[k, step - 1],
                    recv_sem=share_recv.at[k, step - 1],
                    device_id=(comp, lax.rem(harm + step, harm_size)),
                    device_id_type=MESH,
                )
            )
            sends[-1].start()

        @pl.when(has_next)
        def _():
            up.wait_send()
            down.wait_recv()
            ext[pl.ds(BAND + block_rows, BAND)] = halo[k, 1]

        @pl.when(has_prev)
        def _():
            down.wait_send()
            up.wait_recv()
            ext[pl.ds(0, BAND)] = halo[k, 0]

        gathered = span(0, 1, gathered)
        gathered = span(chunks - 1, chunks, gathered)

        if k == 0:
            for copy in table_copies:
                copy.wait()
        for send in sends:
            send.wait()
        for part in range(harm_size):
            high, low = halves(shared[k, part])
            for copy in range(2):
                rel_high[pl.ds(copy * H + part * nh, nh), :] = high
                rel_low[pl.ds(copy * H + part * nh, nh), :] = low
        total = jnp.zeros((2 * nh, cmax), F32)
        extra = jnp.zeros((nh, cmax), F32)
        step_points = 2 * H
        for t in range(0, TIME_POINTS, step_points):
            rows_now = time_ref[pl.ds(t, step_points), :]
            values = product(rows_now, rel_high[...], NN) + product(rows_now, rel_low[...], NN)
            high, low = halves(jnp.tanh(values))
            back = back_ref[harm, :, pl.ds(t, step_points)]
            total = total + product(back, high, NN)
            extra = extra + product(back[:nh], low, NN)
        force = (folded(total) + extra) * own_weight * slot_scale
        projected = stacked(force)
        if not last:
            swap_out[k + 1] = swap_out[k] + (folded(gathered) - force) * slot_inverse[...]
            swap_copy(k + 1).start()

        def finish(p, carry):
            nonlinear = folded(product(projected, hot[lanes(p), :], NT))
            residual = shift[p] - nonlinear
            value = field[p] + residual * inv_ref[p]
            if last:
                disp_out[:, lanes(p)] = value
                res_out[:, lanes(p)] = residual
            else:
                field[p] = value
                put_rounded(p, value)
            return carry

        lax.fori_loop(0, pairs, finish, 0, unroll=4)


def local(comp_size, harm_size, *arrays):
    load, stiff_blocks, mass_blocks, block_cols = arrays[:4]
    nh, dofs = load.shape
    block_rows, slots, blk, _ = stiff_blocks.shape
    cmax = arrays[4].shape[1]
    to_time, back = host_tables(harm_size)
    vmem = pl.BlockSpec(memory_space=pltpu.VMEM)
    smem = pl.BlockSpec(memory_space=pltpu.SMEM)
    hbm = pl.BlockSpec(memory_space=pl.ANY)
    wide = (block_rows // 2, nh, 2 * blk)
    dma = pltpu.SemaphoreType.DMA
    return pl.pallas_call(
        functools.partial(kernel, comp_size, harm_size),
        out_shape=(jax.ShapeDtypeStruct((nh, dofs), F32),) * 2,
        in_specs=[hbm, hbm, hbm, smem, vmem, vmem, smem, vmem, vmem, smem, hbm, hbm],
        out_specs=(vmem, vmem),
        scratch_shapes=[
            pltpu.VMEM(load.shape, F32),
            pltpu.VMEM(to_time.shape, BF16),
            pltpu.VMEM(back.shape, BF16),
            pltpu.VMEM(stiff_blocks.shape, BF16),
            pltpu.VMEM(mass_blocks.shape, BF16),
            pltpu.VMEM(wide, F32),
            pltpu.VMEM(wide, F32),
            pltpu.VMEM(wide, F32),
            pltpu.VMEM(wide, F32),
            pltpu.VMEM((nh, cmax), F32),
            pltpu.VMEM((dofs, cmax), BF16),
            pltpu.VMEM((cmax, cmax), BF16),
            pltpu.VMEM((block_rows + 2 * BAND, nh, blk), BF16),
            pltpu.VMEM((ITERS, 2, BAND, nh, blk), BF16),
            pltpu.VMEM((ITERS, nh, cmax), F32),
            pltpu.VMEM((ITERS, nh, cmax), F32),
            pltpu.VMEM((ITERS, harm_size, nh, cmax), F32),
            pltpu.VMEM((2 * H, cmax), BF16),
            pltpu.VMEM((2 * H, cmax), BF16),
            dma((3,)),
            dma((2,)),
            dma((block_rows // BAND, 2)),
            dma((ITERS, 2)),
            dma((ITERS, 2)),
            dma((ITERS,)),
            dma((ITERS,)),
            dma((ITERS, harm_size - 1)),
            dma((ITERS, harm_size - 1)),
        ],
        compiler_params=pltpu.CompilerParams(
            collective_id=0, has_side_effects=True, vmem_limit_bytes=52 * 1024 * 1024
        ),
    )(load, stiff_blocks, mass_blocks, block_cols.T, *arrays[4:], jnp.asarray(to_time), jnp.asarray(back))


def solution(mesh):
    placed = (
        P("harm", "comp"),
        P("comp", None, None, None),
        P("comp", None, None, None),
        P("comp", None),
        P("comp", None),
        P("comp", None),
        P("comp"),
        P("comp", None),
        P("comp", None),
        P(),
    )
    return jax.shard_map(
        functools.partial(local, mesh.shape["comp"], mesh.shape["harm"]),
        mesh=mesh,
        in_specs=placed,
        out_specs=(P("harm", "comp"), P("harm", "comp")),
        check_vma=False,
    )
```

```python
import functools
import math

import jax
import jax.numpy as jnp
import numpy as np
from jax import lax
from jax.experimental import pallas as pl
from jax.experimental.pallas import tpu as pltpu
from jax.sharding import PartitionSpec as P

H = 128
TIME_POINTS = 1024
BAND = 8
ITERS = 3
MESH = pl.DeviceIdType.MESH
F32 = jnp.float32
BF16 = jnp.bfloat16
NN = (((1,), (0,)), ((), ()))
NT = (((1,), (1,)), ((), ()))


def host_tables(harm_parts):
    column = np.arange(H)
    orders = np.where(column <= H // 2, column, column - H // 2)
    phase = np.arange(TIME_POINTS)[:, None] * orders[None, :] % TIME_POINTS
    angle = phase * (2.0 * math.pi / TIME_POINTS)
    table = np.where(column[None, :] <= H // 2, np.cos(angle), np.sin(angle))
    table = table.astype(np.float32)
    high = table.astype(BF16)
    low = (table - high.astype(np.float32)).astype(BF16)
    to_time = np.concatenate([high, low], axis=1)
    back = np.stack(
        [high.T.reshape(harm_parts, -1, TIME_POINTS), low.T.reshape(harm_parts, -1, TIME_POINTS)], axis=1
    )
    return to_time, back.reshape(harm_parts, -1, TIME_POINTS)


def halves(value):
    high = value.astype(BF16)
    low = (value - high.astype(F32)).astype(BF16)
    return high, low


def stacked(value):
    return jnp.concatenate(halves(value), axis=0)


def folded(value):
    half = value.shape[0] // 2
    return value[:half] + value[half:]


def product(left, right, dims):
    return lax.dot_general(left, right, dims, preferred_element_type=F32)


def kernel(
    comp_size,
    harm_size,
    load_hbm,
    stiff_hbm,
    mass_hbm,
    cols_hbm,
    rows_hbm,
    partner_hbm,
    count_ref,
    normal_hbm,
    spring_hbm,
    freq_ref,
    time_hbm,
    back_hbm,
    disp_out,
    res_out,
    cols_ref,
    rows_ref,
    partner_ref,
    normal_ref,
    spring_ref,
    factor_ref,
    load_ref,
    time_ref,
    back_ref,
    stiff_ref,
    mass_ref,
    field,
    shift,
    dyn_ref,
    inv_ref,
    slot_inverse,
    hot,
    perm,
    ext,
    halo,
    swap_out,
    swap_in,
    shared,
    rel_high,
    rel_low,
    small_sem,
    side_sem,
    diag_sem,
    block_sem,
    halo_send,
    halo_recv,
    swap_send,
    swap_recv,
    share_send,
    share_recv,
):
    comp = lax.axis_index("comp")
    harm = lax.axis_index("harm")
    block_rows = stiff_ref.shape[0]
    slots = stiff_ref.shape[1]
    blk = stiff_ref.shape[2]
    nh = load_ref.shape[0]
    wide = 2 * blk
    pairs = block_rows // 2
    chunks = block_rows // BAND
    cmax = rows_ref.shape[1]
    first_row = comp * block_rows
    has_prev = comp > 0
    has_next = comp < comp_size - 1
    after = lax.rem(comp + 1, comp_size)
    before = lax.rem(comp + comp_size - 1, comp_size)
    facing = lax.rem(comp + comp_size // 2, comp_size)
    order = list(range(1, chunks - 1)) + [0, chunks - 1]

    small_copies = [
        pltpu.make_async_copy(source, held, small_sem.at[i])
        for i, (source, held) in enumerate(
            (
                (rows_hbm, rows_ref),
                (partner_hbm, partner_ref),
                (normal_hbm, normal_ref),
                (spring_hbm, spring_ref),
                (cols_hbm, cols_ref),
            )
        )
    ]
    for copy in small_copies:
        copy.start()
    diag_copies = [
        pltpu.make_async_copy(source.at[:, pl.ds(0, 1)], held.at[:, pl.ds(0, 1)], diag_sem.at[i])
        for i, (source, held) in enumerate(((stiff_hbm, stiff_ref), (mass_hbm, mass_ref)))
    ]
    for copy in diag_copies:
        copy.start()
    load_copy, *table_copies = [
        pltpu.make_async_copy(source, held, side_sem.at[i])
        for i, (source, held) in enumerate(
            ((load_hbm, load_ref), (time_hbm, time_ref), (back_hbm, back_ref))
        )
    ]
    load_copy.start()
    block_copies = {}
    for c in order:
        span = (pl.ds(c * BAND, BAND), pl.ds(1, slots - 1))
        block_copies[c] = [
            pltpu.make_async_copy(source.at[span], held.at[span], block_sem.at[c, i])
            for i, (source, held) in enumerate(((stiff_hbm, stiff_ref), (mass_hbm, mass_ref)))
        ]
        for copy in block_copies[c]:
            copy.start()
    for copy in table_copies:
        copy.start()

    barrier = pltpu.get_barrier_semaphore()
    pl.semaphore_signal(barrier, inc=1, device_id=(facing, harm), device_id_type=MESH)
    for step in range(1, harm_size):
        peer = lax.rem(harm + step, harm_size)
        pl.semaphore_signal(barrier, inc=1, device_id=(comp, peer), device_id_type=MESH)

    @pl.when(has_prev)
    def _():
        pl.semaphore_signal(barrier, inc=1, device_id=(before, harm), device_id_type=MESH)

    @pl.when(has_next)
    def _():
        pl.semaphore_signal(barrier, inc=1, device_id=(after, harm), device_id_type=MESH)

    for copy in small_copies:
        copy.wait()

    row_list = rows_ref[...]
    sub = lax.broadcasted_iota(jnp.int32, (wide, cmax), 0)

    def mark(p, carry):
        base = pl.multiple_of(p * wide, wide)
        hot[pl.ds(base, wide), :] = jnp.where(sub == row_list - base, 1.0, 0.0).astype(BF16)
        return carry

    lax.fori_loop(0, pairs, mark, 0, unroll=2)
    slot_axis = lax.broadcasted_iota(jnp.int32, (cmax, cmax), 0)
    perm[...] = jnp.where(slot_axis == partner_ref[...], 1.0, 0.0).astype(BF16)
    ext[pl.ds(0, BAND)] = jnp.zeros((BAND, nh, blk), BF16)
    ext[pl.ds(BAND + block_rows, BAND)] = jnp.zeros((BAND, nh, blk), BF16)

    def factor_of(width):
        index = harm * nh + lax.broadcasted_iota(jnp.int32, (nh, width), 0)
        wave = jnp.where(index <= H // 2, index, index - H // 2).astype(F32)
        value = freq_ref[0] * wave * (2.0 / H)
        return value * value

    factor_ref[...] = factor_of(wide)
    slot_index = lax.broadcasted_iota(jnp.int32, (1, cmax), 1)
    slot_scale = jnp.where(slot_index < count_ref[0], normal_ref[...], 0.0)
    own_index = harm * nh + lax.broadcasted_iota(jnp.int32, (nh, cmax), 0)
    own_weight = jnp.where(own_index == 0, 1.0 / TIME_POINTS, 2.0 / TIME_POINTS)
    spring_ratio = spring_ref[...] / normal_ref[...]

    for copy in diag_copies:
        copy.wait()
    load_copy.wait()
    eye = lax.broadcasted_iota(jnp.int32, (blk, blk), 0) == lax.broadcasted_iota(
        jnp.int32, (blk, blk), 1
    )

    def diagonal(ref, p):
        parts = [
            jnp.sum(jnp.where(eye, ref[2 * p + q, 0].astype(F32), 0.0), axis=0, keepdims=True)
            for q in range(2)
        ]
        return jnp.concatenate(parts, axis=1)

    def put_rounded(p, value):
        rounded = value.astype(BF16)
        for q in range(2):
            ext[BAND + 2 * p + q] = rounded[:, q * blk : (q + 1) * blk]

    def lanes(p):
        return pl.ds(pl.multiple_of(p * wide, wide), wide)

    def start_field(p, gathered):
        stiff_diag = diagonal(stiff_ref, p)
        mass_diag = diagonal(mass_ref, p)
        dynamic = stiff_diag - factor_ref[...] * mass_diag
        inverse = 1.0 / dynamic
        value = load_ref[:, lanes(p)] * inverse
        dyn_ref[p] = dynamic
        inv_ref[p] = inverse
        field[p] = value
        put_rounded(p, value)
        high, low = halves(value)
        diagonals = jnp.concatenate(
            [jnp.broadcast_to(part, (8, wide)) for part in (stiff_diag, mass_diag)], axis=0
        )
        left = jnp.concatenate([high, low, diagonals.astype(BF16)], axis=0)
        return gathered + product(left, hot[lanes(p), :], NN)

    gathered = lax.fori_loop(
        0, pairs, start_field, jnp.zeros((2 * nh + 16, cmax), F32), unroll=4
    )
    listed = folded(gathered[: 2 * nh])
    slot_dynamic = gathered[2 * nh : 2 * nh + 1] - factor_of(cmax) * gathered[2 * nh + 8 : 2 * nh + 9]
    slot_inverse[...] = 1.0 / slot_dynamic

    neighbours = jnp.minimum(comp, 1) + jnp.minimum(comp_size - 1 - comp, 1)
    pl.semaphore_wait(barrier, harm_size + neighbours)

    def apply_rows(first, stop, gathered):
        def body(p, carry):
            applied = []
            for q in range(2):
                r = 2 * p + q
                picked = jnp.concatenate(
                    [
                        ext[jnp.clip(cols_ref[s, r] - first_row + BAND, 0, ext.shape[0] - 1)]
                        for s in range(slots)
                    ],
                    axis=1,
                )
                blocks = jnp.concatenate(
                    [
                        jnp.concatenate([ref[r, s] for s in range(slots)], axis=1)
                        for ref in (stiff_ref, mass_ref)
                    ],
                    axis=0,
                )
                both = product(picked, blocks, NT)
                applied.append(both[:, :blk] - factor_ref[:, :blk] * both[:, blk:])
            rounded = jnp.concatenate([ext[BAND + 2 * p + q] for q in range(2)], axis=1)
            gap = field[p] - rounded.astype(F32)
            value = load_ref[:, lanes(p)] - jnp.concatenate(applied, axis=1) - dyn_ref[p] * gap
            shift[p] = value
            if carry is None:
                return carry
            return carry + product(stacked(value), hot[lanes(p), :], NN)

        return lax.fori_loop(first * BAND // 2, stop * BAND // 2, body, gathered, unroll=4)

    def swap_copy(k):
        return pltpu.make_async_remote_copy(
            src_ref=swap_out.at[k],
            dst_ref=swap_in.at[k],
            send_sem=swap_send.at[k],
            recv_sem=swap_recv.at[k],
            device_id=(facing, harm),
            device_id_type=MESH,
        )

    def halo_copies(k):
        up = pltpu.make_async_remote_copy(
            src_ref=ext.at[pl.ds(block_rows, BAND)],
            dst_ref=halo.at[k, 0],
            send_sem=halo_send.at[k, 0],
            recv_sem=halo_recv.at[k, 0],
            device_id=(after, harm),
            device_id_type=MESH,
        )
        down = pltpu.make_async_remote_copy(
            src_ref=ext.at[pl.ds(BAND, BAND)],
            dst_ref=halo.at[k, 1],
            send_sem=halo_send.at[k, 1],
            recv_sem=halo_recv.at[k, 1],
            device_id=(before, harm),
            device_id_type=MESH,
        )
        return up, down

    def start_halo(k):
        up, down = halo_copies(k)

        @pl.when(has_next)
        def _():
            up.start()

        @pl.when(has_prev)
        def _():
            down.start()

    swap_out[0] = listed
    swap_copy(0).start()
    start_halo(0)

    for k in range(ITERS):
        up, down = halo_copies(k)
        last = k == ITERS - 1

        def span(first, stop, gathered):
            if k > 0:
                return apply_rows(first, stop, gathered)
            for chunk in range(first, stop):
                for copy in block_copies[chunk]:
                    copy.wait()
                gathered = apply_rows(chunk, chunk + 1, gathered)
            return gathered

        gathered = None if last else jnp.zeros((2 * nh, cmax), F32)
        gathered = span(1, chunks - 1, gathered)

        swap_copy(k).wait()
        mirrored = folded(product(stacked(swap_in[k]), perm[...], NN))
        shared[k, harm] = (swap_out[k] - mirrored) * spring_ratio
        sends = []
        for step in range(1, harm_size):
            sends.append(
                pltpu.make_async_remote_copy(
                    src_ref=shared.at[k, harm],
                    dst_ref=shared.at[k, harm],
                    send_sem=share_send.at[k, step - 1],
                    recv_sem=share_recv.at[k, step - 1],
                    device_id=(comp, lax.rem(harm + step, harm_size)),
                    device_id_type=MESH,
                )
            )
            sends[-1].start()

        @pl.when(has_next)
        def _():
            up.wait_send()
            down.wait_recv()
            ext[pl.ds(BAND + block_rows, BAND)] = halo[k, 1]

        @pl.when(has_prev)
        def _():
            down.wait_send()
            up.wait_recv()
            ext[pl.ds(0, BAND)] = halo[k, 0]

        gathered = span(0, 1, gathered)
        gathered = span(chunks - 1, chunks, gathered)

        if k == 0:
            for copy in table_copies:
                copy.wait()
        for send in sends:
            send.wait()
        for part in range(harm_size):
            high, low = halves(shared[k, part])
            for copy in range(2):
                rel_high[pl.ds(copy * H + part * nh, nh), :] = high
                rel_low[pl.ds(copy * H + part * nh, nh), :] = low
        total = jnp.zeros((2 * nh, cmax), F32)
        extra = jnp.zeros((nh, cmax), F32)
        step_points = 2 * H
        for t in range(0, TIME_POINTS, step_points):
            rows_now = time_ref[pl.ds(t, step_points), :]
            values = product(rows_now, rel_high[...], NN) + product(rows_now, rel_low[...], NN)
            high, low = halves(jnp.tanh(values))
            back = back_ref[harm, :, pl.ds(t, step_points)]
            total = total + product(back, high, NN)
            extra = extra + product(back[:nh], low, NN)
        force = (folded(total) + extra) * own_weight * slot_scale
        projected = stacked(force)
        if not last:
            swap_out[k + 1] = swap_out[k] + (folded(gathered) - force) * slot_inverse[...]
            swap_copy(k + 1).start()

        def finish(p, carry):
            nonlinear = folded(product(projected, hot[lanes(p), :], NT))
            residual = shift[p] - nonlinear
            value = field[p] + residual * inv_ref[p]
            if last:
                disp_out[:, lanes(p)] = value
                res_out[:, lanes(p)] = residual
            else:
                field[p] = value
                put_rounded(p, value)
            return carry

        edge = BAND // 2
        lax.fori_loop(0, edge, finish, 0, unroll=edge)
        lax.fori_loop(pairs - edge, pairs, finish, 0, unroll=edge)
        if not last:
            start_halo(k + 1)
        lax.fori_loop(edge, pairs - edge, finish, 0, unroll=8)


def local(comp_size, harm_size, *arrays):
    load, stiff_blocks, mass_blocks, block_cols = arrays[:4]
    nh, dofs = load.shape
    block_rows, slots, blk, _ = stiff_blocks.shape
    cmax = arrays[4].shape[1]
    to_time, back = host_tables(harm_size)
    vmem = pl.BlockSpec(memory_space=pltpu.VMEM)
    smem = pl.BlockSpec(memory_space=pltpu.SMEM)
    hbm = pl.BlockSpec(memory_space=pltpu.HBM)
    wide = (block_rows // 2, nh, 2 * blk)
    dma = pltpu.SemaphoreType.DMA
    return pl.pallas_call(
        functools.partial(kernel, comp_size, harm_size),
        out_shape=(jax.ShapeDtypeStruct((nh, dofs), F32),) * 2,
        in_specs=[hbm, hbm, hbm, hbm, hbm, hbm, smem, hbm, hbm, smem, hbm, hbm],
        out_specs=(vmem, vmem),
        scratch_shapes=[
            pltpu.SMEM((slots, block_rows), jnp.int32),
            pltpu.VMEM((1, cmax), jnp.int32),
            pltpu.VMEM((1, cmax), jnp.int32),
            pltpu.VMEM((1, cmax), F32),
            pltpu.VMEM((1, cmax), F32),
            pltpu.VMEM((nh, 2 * blk), F32),
            pltpu.VMEM(load.shape, F32),
            pltpu.VMEM(to_time.shape, BF16),
            pltpu.VMEM(back.shape, BF16),
            pltpu.VMEM(stiff_blocks.shape, BF16),
            pltpu.VMEM(mass_blocks.shape, BF16),
            pltpu.VMEM(wide, F32),
            pltpu.VMEM(wide, F32),
            pltpu.VMEM(wide, F32),
            pltpu.VMEM(wide, F32),
            pltpu.VMEM((nh, cmax), F32),
            pltpu.VMEM((dofs, cmax), BF16),
            pltpu.VMEM((cmax, cmax), BF16),
            pltpu.VMEM((block_rows + 2 * BAND, nh, blk), BF16),
            pltpu.VMEM((ITERS, 2, BAND, nh, blk), BF16),
            pltpu.VMEM((ITERS, nh, cmax), F32),
            pltpu.VMEM((ITERS, nh, cmax), F32),
            pltpu.VMEM((ITERS, harm_size, nh, cmax), F32),
            pltpu.VMEM((2 * H, cmax), BF16),
            pltpu.VMEM((2 * H, cmax), BF16),
            dma((5,)),
            dma((3,)),
            dma((2,)),
            dma((block_rows // BAND, 2)),
            dma((ITERS, 2)),
            dma((ITERS, 2)),
            dma((ITERS,)),
            dma((ITERS,)),
            dma((ITERS, harm_size - 1)),
            dma((ITERS, harm_size - 1)),
        ],
        compiler_params=pltpu.CompilerParams(
            collective_id=0, has_side_effects=True, vmem_limit_bytes=52 * 1024 * 1024
        ),
    )(load, stiff_blocks, mass_blocks, block_cols.T, *arrays[4:], jnp.asarray(to_time), jnp.asarray(back))


def solution(mesh):
    placed = (
        P("harm", "comp"),
        P("comp", None, None, None),
        P("comp", None, None, None),
        P("comp", None),
        P("comp", None),
        P("comp", None),
        P("comp"),
        P("comp", None),
        P("comp", None),
        P(),
    )
    return jax.shard_map(
        functools.partial(local, mesh.shape["comp"], mesh.shape["harm"]),
        mesh=mesh,
        in_specs=placed,
        out_specs=(P("harm", "comp"), P("harm", "comp")),
        check_vma=False,
    )
```
